32 devices in a mesh: gx: 4 (over z), gy: 4 (over y, x), gz: 2 (over core).
Axes of the slice: x: 2, y: 2, z: 4, core: 2. Of those that a mesh axis runs over, the one named last changes fastest.
Arguments:
- forcing: float32 [3, 64, 64, 256], P(None, 'gx', 'gy', 'gz'), may hold values from -6 to 6
- start_field: float32 [3, 64, 64, 256], P(None, 'gx', 'gy', 'gz'), may hold values from -6 to 6
- modulus: float32 [64, 64, 256], P('gx', 'gy', 'gz'), may hold values from 1 to 4
- corners: int32 [32, 3], P(('gx', 'gy', 'gz')), may hold values from 0 to 236, as said below
Outputs:
- displacement: float32 [3, 64, 64, 256], P(None, 'gx', 'gy', 'gz')
- new_modulus: float32 [64, 64, 256], P('gx', 'gy', 'gz')
The draws below stay inside these ranges and needn't reach their ends.
Inputs may be any that keep to these rules, and one draw needn't show every extreme that they name: `corners`: subzone i is handled by device i // 1 in row-major order over (gx, gy, gz). In each dimension its corner lies within lo - 5 to lo + B + 5 - 2 * 10, where lo and B are that device's first voxel and voxel count in that dimension, and the subzone lies inside the grid.
All inputs are finite; a program needn't handle non-finite values.
Results may differ from the reference program's by a relative error of at most 0.0003.
Values sent between devices are 32-bit elements; how exact they have to be, the bound alone decides.
A program may use at most 192 MiB of HBM per device.

```python
import math
import jax
import jax.numpy as jnp
from jax import lax

BX = 16
BY = 16
BZ = 128
SUB_DEV = 1
PC = 10
HALO = 6
FSWEEPS = 4
NX = 64
NY = 64
NZ = 256
NSUB = 32
N_GY = 4
N_GZ = 2


def draw_corners(key, part):
    number = jnp.arange(NSUB, dtype=jnp.int32)
    device = number // SUB_DEV
    brick_x = device // (N_GY * N_GZ)
    brick_y = device // N_GZ % N_GY
    brick_z = device % N_GZ
    lower = jnp.stack([brick_x * BX, brick_y * BY, brick_z * BZ], axis=1)
    counts = jnp.array([BX + 2 * HALO - 1 - 2 * PC, BY + 2 * HALO - 1 - 2 * PC, BZ + 2 * HALO - 1 - 2 * PC], jnp.int32)
    offsets = jax.random.randint(key, (NSUB, 3), jnp.zeros((1, 3), jnp.int32), counts[None, :])
    corner_raw = lower - HALO + 1 + offsets
    upper_limit = jnp.array([NX, NY, NZ], jnp.int32) - 2 * PC
    return jnp.clip(corner_raw, 0, upper_limit[None, :]).astype(jnp.int32)


def block_amplitude(key):
    cell_x = (NX + 3) // 4
    cell_y = (NY + 3) // 4
    cell_z = (NZ + 3) // 4
    exponent = jax.random.uniform(jax.random.fold_in(key, 11), (cell_x, cell_y, cell_z), jnp.float32, -4.0, 0.0)
    amplitude = jnp.exp(exponent)
    amplitude = jnp.repeat(jnp.repeat(jnp.repeat(amplitude, 4, axis=0), 4, axis=1), 4, axis=2)
    return amplitude[:NX, :NY, :NZ]


def modulated_field(key, draw_tag):
    amplitude = block_amplitude(key)
    inner_key = jax.random.fold_in(key, draw_tag)
    samples = jax.random.normal(inner_key, (3, NX, NY, NZ), jnp.float32)
    return jnp.clip(samples * amplitude[None], -6.0, 6.0).astype(jnp.float32)


def draw_forcing(key, part):
    return modulated_field(key, 21)


def draw_start_field(key, part):
    return modulated_field(key, 37)


def shard_levels(stream_key, extent, split, low, largest):
    factor_of, own = 1.0, jax.random.fold_in(stream_key, 6)
    for dim, shards_of in split:
        steps = jnp.exp(jax.random.uniform(jax.random.fold_in(own, dim), (shards_of,), jnp.float32, low / len(split), largest / len(split)))
        factor_of = factor_of * jnp.repeat(steps, extent[dim] // shards_of).reshape([-1 if axis == dim else 1 for axis in range(len(extent))])
    return factor_of


def setup_inputs(seed: int = 0) -> dict:
    arg_keys = jax.random.split(jax.random.key(seed), 5)
    forcing = draw_forcing(jax.random.fold_in(arg_keys[4], 71), 0)
    start_field = draw_start_field(jax.random.fold_in(arg_keys[4], 71), 0)
    modulus = jnp.clip(jnp.exp(math.log(4.0) - 1.3862944 * jax.random.uniform(arg_keys[2], (NX, NY, NZ), jnp.float32) ** shard_levels(arg_keys[2], (NX, NY, NZ), ((0, 4), (1, 4), (2, 2)), -0.2, 0.2)), 1.0, 4.0)
    corners = draw_corners(jax.random.fold_in(arg_keys[4], 71), 0)
    return dict(forcing=forcing, start_field=start_field, modulus=modulus, corners=corners)


MASS_TERM = 0.5
DAMPING = 0.1
EPSILON = 1e-06
DIRECTIONS = ((0, True), (0, False), (1, True), (1, False), (2, True), (2, False))

def neighbor(values, which_axis, upward):
    index_list = [slice(1, -1), slice(1, -1), slice(1, -1)]
    index_list[which_axis] = slice(2, None) if upward else slice(0, -2)
    return values[tuple([slice(None)] * (values.ndim - 3) + index_list)]

def center(values):
    return values[tuple([slice(None)] * (values.ndim - 3) + [slice(1, -1)] * 3)]

def relax_sweep(field_pad, modulus_pad, forcing_mid):
    middle = center(modulus_pad)
    numerator = forcing_mid
    denominator = MASS_TERM
    for which_axis, upward in DIRECTIONS:
        coupling = 0.5 * (middle + neighbor(modulus_pad, which_axis, upward))
        numerator = numerator + coupling * neighbor(field_pad, which_axis, upward)
        denominator = denominator + coupling
    return numerator / denominator

def block_sum(values, coarse):
    return values.reshape(values.shape[0], coarse, 2, coarse, 2, coarse, 2).sum(axis=(2, 4, 6))

def shift_coarse(values, offset):
    padded = jnp.pad(values, 1)
    coarse = values.shape[0]
    begin = (1 - offset[0], 1 - offset[1], 1 - offset[2])
    return lax.slice(padded, begin, (begin[0] + coarse, begin[1] + coarse, begin[2] + coarse))

def zone_update(field_rim, forcing_zone, modulus_rim):
    zone_span = forcing_zone.shape[-1]
    coarse = zone_span // 2
    params = coarse ** 3
    field_mid = center(field_rim)
    modulus_mid = center(modulus_rim)
    applied = MASS_TERM * field_mid
    laplace = jnp.zeros_like(field_mid)
    face_flows = []
    for which_axis, upward in DIRECTIONS:
        field_next = neighbor(field_rim, which_axis, upward)
        modulus_next = neighbor(modulus_rim, which_axis, upward)
        change = field_mid - field_next
        applied = applied + 0.5 * (modulus_mid + modulus_next) * change
        laplace = laplace + change
        face_flows.append(-0.5 * modulus_next * change)
    coarse_resid = block_sum(forcing_zone - applied, coarse)
    diagonal = block_sum(-0.5 * modulus_mid * laplace, coarse)
    position = jnp.arange(coarse)
    columns = {}
    for (which_axis, upward), face_flow in zip(DIRECTIONS, face_flows):
        blocks = face_flow.reshape(3, coarse, 2, coarse, 2, coarse, 2)
        inner_pos = 0 if upward else 1
        same_part = lax.index_in_dim(blocks, inner_pos, 2 + 2 * which_axis, keepdims=True).sum(axis=(2, 4, 6))
        cross_part = lax.index_in_dim(blocks, 1 - inner_pos, 2 + 2 * which_axis, keepdims=True).sum(axis=(2, 4, 6))
        diagonal = diagonal + same_part
        in_range = position < coarse - 1 if upward else position > 0
        shape_list = [1, 1, 1]
        shape_list[which_axis] = coarse
        in_range = in_range.reshape(shape_list)
        step_list = [0, 0, 0]
        step_list[which_axis] = 1 if upward else -1
        columns[tuple(step_list)] = jnp.where(in_range, cross_part, 0.0)
    columns[0, 0, 0] = diagonal
    offset_list = list(columns.keys())
    gradient = jnp.zeros((coarse, coarse, coarse), jnp.float32)
    band_sums = {}
    for offset_one in offset_list:
        gradient = gradient + shift_coarse(jnp.sum(columns[offset_one] * coarse_resid, axis=0), offset_one)
        for offset_two in offset_list:
            band_key = (offset_two[0] - offset_one[0], offset_two[1] - offset_one[1], offset_two[2] - offset_one[2])
            term_value = shift_coarse(jnp.sum(columns[offset_one] * columns[offset_two], axis=0), offset_one)
            if band_key in band_sums:
                band_sums[band_key] = band_sums[band_key] + term_value
            else:
                band_sums[band_key] = term_value
    base_rows = jnp.arange(params, dtype=jnp.int32)
    row_parts = []
    col_parts = []
    value_parts = []
    for band_key, band_value in band_sums.items():
        linear = band_key[0] * coarse * coarse + band_key[1] * coarse + band_key[2]
        target = base_rows + linear
        target = jnp.where((target >= 0) & (target < params), target, params).astype(jnp.int32)
        row_parts.append(base_rows)
        col_parts.append(target)
        value_parts.append(band_value.reshape(params))
    hessian = jnp.zeros((params, params), jnp.float32).at[jnp.concatenate(row_parts), jnp.concatenate(col_parts)].add(jnp.concatenate(value_parts), mode='drop')
    ridge = DAMPING * jnp.sum(band_sums[0, 0, 0]) / params + EPSILON
    hessian = hessian + ridge * jnp.eye(params, dtype=jnp.float32)
    factor = jnp.linalg.cholesky(hessian)
    right_hand = gradient.reshape(params, 1)
    middle_sol = lax.linalg.triangular_solve(factor, right_hand, left_side=True, lower=True)
    solution = lax.linalg.triangular_solve(factor, middle_sol, left_side=True, lower=True, transpose_a=True)
    update = -solution.reshape(coarse, coarse, coarse)
    update = jnp.repeat(jnp.repeat(jnp.repeat(update, 2, axis=0), 2, axis=1), 2, axis=2)
    ramp_curve = jnp.sin(math.pi * (jnp.arange(zone_span, dtype=jnp.float32) + 0.5) / zone_span)
    taper_weight = ramp_curve[:, None, None] * ramp_curve[None, :, None] * ramp_curve[None, None, :]
    return taper_weight * modulus_mid * update

def reference(forcing, start_field, modulus, corners):
    zone_span = 2 * PC
    field = start_field
    modulus_pad = jnp.pad(modulus, 1)
    for sweep_count in range(FSWEEPS):
        field = relax_sweep(jnp.pad(field, ((0, 0), (1, 1), (1, 1), (1, 1))), modulus_pad, forcing)
    field_pad = jnp.pad(field, ((0, 0), (1, 1), (1, 1), (1, 1)))
    anchor = jnp.zeros((), jnp.int32)

    def one_zone(corner):
        corner = corner.astype(jnp.int32)
        field_rim = lax.dynamic_slice(field_pad, (anchor, corner[0], corner[1], corner[2]), (3, zone_span + 2, zone_span + 2, zone_span + 2))
        modulus_rim = lax.dynamic_slice(modulus_pad, (corner[0], corner[1], corner[2]), (zone_span + 2, zone_span + 2, zone_span + 2))
        forcing_zone = lax.dynamic_slice(forcing, (anchor, corner[0], corner[1], corner[2]), (3, zone_span, zone_span, zone_span))
        return zone_update(field_rim, forcing_zone, modulus_rim)
    pieces = lax.map(one_zone, corners)

    def add_piece(number, total):
        corner = corners[number].astype(jnp.int32)
        begin = (corner[0], corner[1], corner[2])
        current = lax.dynamic_slice(total, begin, (zone_span, zone_span, zone_span))
        return lax.dynamic_update_slice(total, current + pieces[number], begin)
    total = lax.fori_loop(0, corners.shape[0], add_piece, jnp.zeros(modulus.shape, jnp.float32))
    return (field, modulus + total)
```

```python
import functools
import math

import jax
import jax.numpy as jnp
from jax import lax
from jax.experimental import pallas as pl
from jax.experimental.pallas import tpu as pltpu
from jax.sharding import PartitionSpec as P

PC = 10
HALO = 6
FSWEEPS = 4


MASS_TERM = 0.5
DAMPING = 0.1
EPSILON = 1e-06
HIGHEST = lax.Precision.HIGHEST
F32 = jnp.float32


def extended(block, sides, width):
    for axis, dim in sides:
        count = lax.axis_size(axis)
        forward = [(i, i + 1) for i in range(count - 1)]
        backward = [(target, source) for source, target in forward]
        low = lax.ppermute(
            lax.slice_in_dim(block, block.shape[dim] - width, None, axis=dim), axis, forward
        )
        high = lax.ppermute(lax.slice_in_dim(block, 0, width, axis=dim), axis, backward)
        block = jnp.concatenate([low, block, high], axis=dim)
    return block


def pack_margins(values, which_axis, margin):
    inner = values.shape[which_axis] - 2 * margin
    return jnp.concatenate(
        [
            lax.slice_in_dim(values, 0, margin, axis=which_axis),
            lax.slice_in_dim(values, 2 * margin, inner, axis=which_axis),
            lax.slice_in_dim(values, inner + margin, inner + 2 * margin, axis=which_axis),
        ],
        axis=which_axis,
    )


def fold_margins(values, received, which_axis, margin):
    inner = values.shape[which_axis] - 2 * margin
    middle_shape = list(values.shape)
    middle_shape[which_axis] = inner - 2 * margin
    added = jnp.concatenate(
        [
            lax.slice_in_dim(received, 0, margin, axis=which_axis),
            jnp.zeros(middle_shape, jnp.float32),
            lax.slice_in_dim(received, inner + margin, inner + 2 * margin, axis=which_axis),
        ],
        axis=which_axis,
    )
    return lax.slice_in_dim(values, margin, inner + margin, axis=which_axis) + added


def dot(a, b, contract):
    return lax.dot_general(
        a, b, ((contract[:1], contract[1:]), ((), ())), precision=HIGHEST, preferred_element_type=F32
    )


def roll(values, shift, axis):
    return pltpu.roll(values, shift % values.shape[axis], axis)


def iota(shape, axis):
    return lax.broadcasted_iota(jnp.int32, shape, axis)


def relax_planes(totals, brick, margin, wide, field_out, buffers, faces):
    _, span_x, rows, lanes = wide.shape
    mx, my, mz, inverse = faces
    low = [lax.axis_index(name) * size - margin for name, size in zip(("gx", "gy", "gz"), brick)]
    y_pos = low[1] + iota((rows, lanes), 0)
    z_pos = low[2] + iota((rows, lanes), 1)
    inside = (y_pos >= 0) & (y_pos < totals[1]) & (z_pos >= 0) & (z_pos < totals[2])

    mx[0] = 0.5 * (wide[6, 0] + wide[6, 1])

    def couple(x, _):
        m = wide[6, x]
        face_z = 0.5 * (m + roll(m, -1, 1))
        face_y = 0.5 * (m + roll(m, -1, 0))
        face_x = 0.5 * (m + wide[6, x + 1])
        mx[x], my[x], mz[x] = face_x, face_y, face_z
        below = MASS_TERM + face_x + mx[x - 1] + face_y + roll(face_y, 1, 0)
        below = below + face_z + roll(face_z, 1, 1)
        x_pos = low[0] + x
        here = inside & (x_pos >= 0) & (x_pos < totals[0])
        inverse[x] = jnp.where(here, 1.0 / below, 0.0)
        return 0

    lax.fori_loop(1, span_x - 1, couple, 0)
    source = wide
    for sweep in range(FSWEEPS):
        target = buffers[sweep % 2]

        def relax(x, _, source=source, target=target):
            face_x, face_y, face_z, before = mx[x], my[x], mz[x], mx[x - 1]
            scale = inverse[x]
            for k in range(3):
                u = source[k, x]
                total = wide[3 + k, x] + face_x * source[k, x + 1] + before * source[k, x - 1]
                total = total + face_y * roll(u, -1, 0) + roll(face_y * u, 1, 0)
                total = total + face_z * roll(u, -1, 1) + roll(face_z * u, 1, 1)
                target[k, x] = total * scale
            return 0

        lax.fori_loop(sweep + 1, span_x - 1 - sweep, relax, 0)
        source = target
    for k in range(3):
        for x in range(brick[0]):
            plane = roll(source[k, margin + x, :, :], -margin, 1)
            field_out[k, x] = plane[margin : margin + brick[1], : brick[2]]
    return source


def cut_zone(begin, source, wide, zone_u, zone_f, zone_m):
    count, rows = zone_m.shape[:2]
    shift = lax.rem(source.shape[-1] - begin[2], source.shape[-1])
    shift_y = lax.rem(source.shape[-2] - begin[1], source.shape[-2])

    def cut(x, _):
        def take(ref, k):
            plane = pltpu.roll(ref[k, begin[0] + x], shift, 1)[:, :128]
            return pltpu.roll(plane, shift_y, 0)[:rows]

        for k in range(3):
            zone_u[k, x] = take(source, k)
            zone_f[k, x] = take(wide, 3 + k)
        zone_m[x] = take(wide, 6)
        return 0

    lax.fori_loop(0, count, cut, 0)


FIELDS = 8


def coarse_fields(zone_u, zone_f, zone_m, temp, fields):
    rows = zone_m.shape[1]
    first_y = iota((rows, 128), 0) % 2 == 1
    first_z = iota((rows, 128), 1) % 2 == 1
    rank = iota((PC, 128), 0)
    lane = iota((PC, 128), 1)
    for x in range(PC):
        for k in range(3):
            sums = [None] * FIELDS

            def put(number, value):
                sums[number] = value if sums[number] is None else sums[number] + value

            for a in range(2):
                at = 2 * x + 1 + a
                u, m = zone_u[k, at], zone_m[at]
                applied = MASS_TERM * u
                laplace = jnp.zeros_like(u)
                for number, (axis, step) in enumerate(
                    ((0, 1), (0, -1), (1, 1), (1, -1), (2, 1), (2, -1))
                ):
                    if axis == 0:
                        u_next, m_next = zone_u[k, at + step], zone_m[at + step]
                    else:
                        u_next, m_next = roll(u, -step, axis - 1), roll(m, -step, axis - 1)
                    change = u - u_next
                    applied = applied + 0.5 * (m + m_next) * change
                    laplace = laplace + change
                    flow = -0.5 * m_next * change
                    if axis == 0:
                        same = (a == 0) == (step == 1)
                        put(0 if same else 1 + number, flow)
                    else:
                        first = first_y if axis == 1 else first_z
                        near = first if step == 1 else ~first
                        put(0, jnp.where(near, flow, 0.0))
                        put(1 + number, jnp.where(near, 0.0, flow))
                put(0, -0.5 * m * laplace)
                put(7, zone_f[k, at] - applied)
            for number in range(FIELDS):
                slot = temp.at[k * FIELDS + number]
                slot[...] = sums[number]
                pair = slot[pl.ds(1, PC, stride=2), :] + slot[pl.ds(2, PC, stride=2), :]
                pair = pair + roll(pair, -1, 1)
                keep = (lane % 2 == 1) & (lane < 2 * PC)
                if number == 1 and x == PC - 1 or number == 2 and x == 0:
                    keep = jnp.zeros_like(keep)
                if number == 3:
                    keep = keep & (rank < PC - 1)
                if number == 4:
                    keep = keep & (rank > 0)
                if number == 5:
                    keep = keep & (lane < 2 * PC - 2)
                if number == 6:
                    keep = keep & (lane > 1)
                fields[k * FIELDS + number, x * PC : (x + 1) * PC, :] = jnp.where(keep, pair, 0.0)


def assemble(fields, strip, mat, side):
    size = fields.shape[1]
    gap = iota((size, 128), 1) - iota((size, 128), 0)
    mat[...] = jnp.zeros_like(mat)
    side[...] = jnp.zeros_like(side)
    for c in range(2):
        for t in range(PC // 2):
            z = t if c == 0 else PC - 1 - t
            for k in range(3):
                def column(number):
                    value = fields[k * FIELDS + number, :, 2 * z + 1 : 2 * z + 2]
                    return jnp.broadcast_to(value, (size, 128))

                part = slice(k * size, (k + 1) * size)
                ahead, behind = (5, 6) if c == 0 else (6, 5)
                strip[part, 0:128] = jnp.where(gap == 0, column(behind), 0.0)
                inner = jnp.where(gap == 0, column(0), 0.0)
                for number, offset in ((1, PC), (2, -PC), (3, 1), (4, -1)):
                    inner = jnp.where(gap == offset, column(number), inner)
                strip[part, 128:256] = inner
                strip[part, 256:384] = jnp.where(gap == 0, column(ahead), 0.0)
                strip[part, 384:512] = column(7)
            product = dot(strip[:, :384], strip[...], (0, 0))
            for i in range(3):
                at = t - 1 + i
                if at < 0:
                    continue
                rows = slice(128 * i, 128 * (i + 1))
                mat[c, at] += product[rows, 128 * i : 128 * (i + 1)]
                for j in range(i + 1, 3):
                    place = slice(128 * (j - i - 1), 128 * (j - i))
                    side[c, at, :, place] += product[rows, 128 * j : 128 * (j + 1)]
                side[c, at, :, 256:384] += product[rows, 384:512]


def inverted(blocks, count):
    row_at = iota(blocks[0].shape, 0)
    lane_at = iota((1, blocks[0].shape[1]), 1)
    for j in range(count):
        done = []
        for block in blocks:
            column = block[:, j : j + 1]
            row = block[j : j + 1, :]
            pivot = 1.0 / row[:, j : j + 1]
            row = jnp.where(lane_at == j, pivot, row * pivot)
            clear = (row_at == j) | (lane_at == j)
            column = jnp.where(row_at == j, -1.0, column)
            done.append(jnp.where(clear, 0.0, block) - column * row)
        blocks = done
    return blocks


def eliminate(t, chains, size, ridge, mat, side, solved):
    params = PC * PC
    diagonal = (iota((size, 128), 0) == iota((size, 128), 1)) & (iota((size, 128), 0) < params)
    blocks = [mat[c, t, :size, :] + jnp.where(diagonal, ridge, 0.0) for c in chains]
    for c, inverse in zip(chains, inverted(blocks, params)):
        right = side[c, t]
        w = dot(inverse, right, (1, 0))
        solved[c, t] = w
        schur = dot(right[:size, :256], w, (0, 0))
        mat[c, t + 1] -= schur[:128, :128]
        side[c, t + 1, :, 0:128] -= schur[:128, 128:256]
        side[c, t + 1, :, 256:384] -= schur[:128, 256:384]
        mat[c, t + 2] -= schur[128:, 128:256]
        side[c, t + 2, :, 256:384] -= schur[128:, 256:384]


def solve_zone(fields, mat, side, solved, answer):
    size = fields.shape[1]
    squares = jnp.zeros((size, 128), F32)
    for number in range(3 * FIELDS):
        if number % FIELDS < FIELDS - 1:
            squares = squares + fields[number] * fields[number]
    trace = jnp.sum(jnp.sum(squares, axis=0, keepdims=True), axis=1, keepdims=True)
    ridge = DAMPING * trace / PC**3 + EPSILON
    meet = PC // 2 - 1

    def both(t, _):
        eliminate(t, (0, 1), size, ridge, mat, side, solved)
        return 0

    lax.fori_loop(0, meet, both, 0)
    mat[0, meet] += mat[1, meet + 1]
    mat[0, meet + 1] += mat[1, meet]
    side[0, meet, :, 0:128] += side[1, meet, :, 0:128].T
    side[0, meet, :, 256:384] += side[1, meet + 1, :, 256:384]
    side[0, meet + 1, :, 256:384] += side[1, meet, :, 256:384]

    def single(t, _):
        eliminate(t, (0,), size, ridge, mat, side, solved)
        return 0

    lax.fori_loop(meet, meet + 2, single, 0)
    answer[...] = jnp.zeros_like(answer)

    def back(t, c):
        value = solved[c, t, :, 256:384]
        value = value - dot(solved[c, t, :, 0:128], answer[c, t + 1], (1, 0))
        value = value - dot(solved[c, t, :, 128:256], answer[c, t + 2], (1, 0))
        answer[c, t, :size, :] = value

    answer[0, meet + 1, :size, :] = solved[0, meet + 1, :, 256:384]
    value = solved[0, meet, :, 256:384]
    answer[0, meet, :size, :] = value - dot(solved[0, meet, :, 0:128], answer[0, meet + 1], (1, 0))
    answer[1, meet] = answer[0, meet + 1]
    answer[1, meet + 1] = answer[0, meet]
    for t in range(meet - 1, -1, -1):
        for c in range(2):
            back(t, c)


def place_zone(begin, zone_m, answer, spread, temp, added):
    rows = zone_m.shape[1]
    span = 2 * PC
    lane = iota((128, 128), 1)
    update = jnp.zeros((128, 128), F32)
    for z in range(PC):
        value = answer[0, z] if z < PC // 2 else answer[1, PC - 1 - z]
        update = jnp.where((lane == 2 * z + 1) | (lane == 2 * z + 2), -value, update)
    spread[...] = update

    def ramp(position):
        value = jnp.sin(math.pi * (position.astype(F32) - 0.5) / span)
        return jnp.where((position >= 1) & (position <= span), value, 0.0)

    weight = ramp(iota((rows, 128), 0)) * ramp(iota((rows, 128), 1))
    temp[0] = jnp.zeros_like(weight)
    for x in range(PC):
        part = spread[x * PC : (x + 1) * PC, :]
        temp[0, pl.ds(1, PC, stride=2), :] = part
        temp[0, pl.ds(2, PC, stride=2), :] = part
        value = weight * temp[0]
        for a in range(2):
            at = 2 * x + 1 + a
            plane = value * math.sin(math.pi * (at - 0.5) / span) * zone_m[at]
            plane = jnp.pad(plane, ((0, added.shape[1] - rows), (0, 0)))
            plane = pltpu.roll(plane, begin[1] - FSWEEPS, 0)
            plane = jnp.pad(plane, ((0, 0), (0, added.shape[2] - 128)))
            plane = pltpu.roll(plane, begin[2] - FSWEEPS, 1)
            added[begin[0] - FSWEEPS + at] += plane


def kernel(totals, brick, margin, starts, wide, field_out, added, *scratch):
    (buf_a, buf_b, mx, my, mz, inverse, zone_u, zone_f, zone_m) = scratch[:9]
    temp, fields, strip, mat, side, solved, answer, spread = scratch[9:]
    source = relax_planes(
        totals, brick, margin, wide, field_out, (buf_a, buf_b), (mx, my, mz, inverse)
    )
    added[...] = jnp.zeros_like(added)
    for number in range(starts.shape[0]):
        begin = [starts[number, axis] for axis in range(3)]
        cut_zone(begin, source, wide, zone_u, zone_f, zone_m)
        fields[...] = jnp.zeros_like(fields)
        coarse_fields(zone_u, zone_f, zone_m, temp, fields)
        assemble(fields, strip, mat, side)
        solve_zone(fields, mat, side, solved, answer)
        place_zone(begin, zone_m, answer, spread, temp, added)


def body(forcing, start_field, modulus, corners):
    brick = modulus.shape
    lower = [lax.axis_index(n) * size for n, size in zip(("gx", "gy", "gz"), brick)]
    totals = [lax.axis_size(n) * size for n, size in zip(("gx", "gy", "gz"), brick)]
    margin = HALO + FSWEEPS
    stacked = jnp.concatenate([start_field, forcing, modulus[None]], axis=0)
    widened = extended(stacked, (("gx", 1), ("gy", 2), ("gz", 3)), margin)
    _, span_x, span_y, span_z = widened.shape
    rows, lanes = -(-span_y // 8) * 8, max(256, -(-span_z // 128) * 128)
    widened = jnp.pad(widened, ((0, 0), (0, 0), (0, rows - span_y), (0, lanes - span_z)))
    starts = (corners - jnp.stack(lower).astype(jnp.int32)[None, :] + margin - 1).astype(jnp.int32)
    zone_span = 2 * PC + 2
    zone_rows = -(-zone_span // 8) * 8
    size = -(-PC * PC // 8) * 8
    planes = PC // 2 + 3
    plane_buffer = pltpu.VMEM((span_x, rows, lanes), F32)
    reach = tuple(size + 2 * HALO for size in brick)
    whole = pl.BlockSpec(memory_space=pltpu.VMEM)
    field, added = pl.pallas_call(
        functools.partial(kernel, totals, brick, margin),
        out_shape=(
            jax.ShapeDtypeStruct(forcing.shape, F32),
            jax.ShapeDtypeStruct((reach[0], rows, lanes), F32),
        ),
        in_specs=[pl.BlockSpec(memory_space=pltpu.SMEM), whole],
        out_specs=(whole, whole),
        scratch_shapes=[
            pltpu.VMEM((3, span_x, rows, lanes), F32),
            pltpu.VMEM((3, span_x, rows, lanes), F32),
            plane_buffer, plane_buffer, plane_buffer, plane_buffer,
            pltpu.VMEM((3, zone_span, zone_rows, 128), F32),
            pltpu.VMEM((3, zone_span, zone_rows, 128), F32),
            pltpu.VMEM((zone_span, zone_rows, 128), F32),
            pltpu.VMEM((3 * FIELDS, zone_rows, 128), F32),
            pltpu.VMEM((3 * FIELDS, size, 128), F32),
            pltpu.VMEM((3 * size, 512), F32),
            pltpu.VMEM((2, planes, 128, 128), F32),
            pltpu.VMEM((2, planes, 128, 384), F32),
            pltpu.VMEM((2, planes, size, 384), F32),
            pltpu.VMEM((2, planes, 128, 128), F32),
            pltpu.VMEM((128, 128), F32),
        ],
        compiler_params=pltpu.CompilerParams(vmem_limit_bytes=56 * 1024 * 1024),
    )(starts, widened)
    summed = added[:, : reach[1], : reach[2]]
    received = extended(pack_margins(summed, 0, HALO), (("gx", 0),), HALO)
    summed = fold_margins(summed, received, 0, HALO)
    received = extended(pack_margins(summed, 1, HALO), (("gy", 1),), HALO)
    summed = fold_margins(summed, received, 1, HALO)
    received = extended(pack_margins(summed, 2, HALO), (("gz", 2),), HALO)
    summed = fold_margins(summed, received, 2, HALO)
    return (field, modulus + summed)


def solution(mesh):
    placed = (
        P(None, "gx", "gy", "gz"),
        P(None, "gx", "gy", "gz"),
        P("gx", "gy", "gz"),
        P(("gx", "gy", "gz"), None),
    )
    return jax.shard_map(
        body,
        mesh=mesh,
        in_specs=placed,
        out_specs=(P(None, "gx", "gy", "gz"), P("gx", "gy", "gz")),
        check_vma=False,
    )
```

```python
import functools
import math

import jax
import jax.numpy as jnp
from jax import lax
from jax.experimental import pallas as pl
from jax.experimental.pallas import tpu as pltpu
from jax.sharding import PartitionSpec as P

PC = 10
HALO = 6
FSWEEPS = 4


MASS_TERM = 0.5
DAMPING = 0.1
EPSILON = 1e-06
HIGHEST = lax.Precision.HIGHEST
F32 = jnp.float32


def extended(block, sides, width):
    for axis, dim in sides:
        count = lax.axis_size(axis)
        forward = [(i, i + 1) for i in range(count - 1)]
        backward = [(target, source) for source, target in forward]
        low = lax.ppermute(
            lax.slice_in_dim(block, block.shape[dim] - width, None, axis=dim), axis, forward
        )
        high = lax.ppermute(lax.slice_in_dim(block, 0, width, axis=dim), axis, backward)
        block = jnp.concatenate([low, block, high], axis=dim)
    return block


def pack_margins(values, which_axis, margin):
    inner = values.shape[which_axis] - 2 * margin
    return jnp.concatenate(
        [
            lax.slice_in_dim(values, 0, margin, axis=which_axis),
            lax.slice_in_dim(values, 2 * margin, inner, axis=which_axis),
            lax.slice_in_dim(values, inner + margin, inner + 2 * margin, axis=which_axis),
        ],
        axis=which_axis,
    )


def fold_margins(values, received, which_axis, margin):
    inner = values.shape[which_axis] - 2 * margin
    middle_shape = list(values.shape)
    middle_shape[which_axis] = inner - 2 * margin
    added = jnp.concatenate(
        [
            lax.slice_in_dim(received, 0, margin, axis=which_axis),
            jnp.zeros(middle_shape, jnp.float32),
            lax.slice_in_dim(received, inner + margin, inner + 2 * margin, axis=which_axis),
        ],
        axis=which_axis,
    )
    return lax.slice_in_dim(values, margin, inner + margin, axis=which_axis) + added


def dot(a, b, contract):
    return lax.dot_general(
        a, b, ((contract[:1], contract[1:]), ((), ())), precision=HIGHEST, preferred_element_type=F32
    )


def roll(values, shift, axis):
    return pltpu.roll(values, shift % values.shape[axis], axis)


def iota(shape, axis):
    return lax.broadcasted_iota(jnp.int32, shape, axis)


def relax_planes(totals, brick, margin, wide, field_out, buffers, faces):
    _, span_x, rows, lanes = wide.shape
    mx, my, mz, inverse = faces
    low = [lax.axis_index(name) * size - margin for name, size in zip(("gx", "gy", "gz"), brick)]
    y_pos = low[1] + iota((rows, lanes), 0)
    lane = iota((rows, lanes), 1)
    z_pos = low[2] + margin + jnp.where(lane < brick[2] + 64, lane, lane - lanes)
    inside = (y_pos >= 0) & (y_pos < totals[1]) & (z_pos >= 0) & (z_pos < totals[2])

    mx[0] = 0.5 * (wide[6, 0] + wide[6, 1])

    def couple(x, _):
        m = wide[6, x]
        face_z = 0.5 * (m + roll(m, -1, 1))
        face_y = 0.5 * (m + roll(m, -1, 0))
        face_x = 0.5 * (m + wide[6, x + 1])
        mx[x], my[x], mz[x] = face_x, face_y, face_z
        below = MASS_TERM + face_x + mx[x - 1] + face_y + roll(face_y, 1, 0)
        below = below + face_z + roll(face_z, 1, 1)
        x_pos = low[0] + x
        here = inside & (x_pos >= 0) & (x_pos < totals[0])
        inverse[x] = jnp.where(here, 1.0 / below, 0.0)
        return 0

    lax.fori_loop(1, span_x - 1, couple, 0)
    source = wide
    for sweep in range(FSWEEPS):
        target = buffers[sweep % 2]

        def relax(x, _, source=source, target=target):
            face_x, face_y, face_z, before = mx[x], my[x], mz[x], mx[x - 1]
            scale = inverse[x]
            for k in range(3):
                u = source[k, x]
                total = wide[3 + k, x] + face_x * source[k, x + 1] + before * source[k, x - 1]
                total = total + face_y * roll(u, -1, 0) + roll(face_y * u, 1, 0)
                total = total + face_z * roll(u, -1, 1) + roll(face_z * u, 1, 1)
                target[k, x] = total * scale
            return 0

        lax.fori_loop(sweep + 1, span_x - 1 - sweep, relax, 0)
        source = target
    for k in range(3):
        for x in range(brick[0]):
            field_out[k, x] = source[k, margin + x, margin : margin + brick[1], : brick[2]]
    return source


def cut_zone(begin, margin, source, wide, zone_u, zone_f, zone_m):
    count, rows = zone_m.shape[:2]
    shift = lax.rem(source.shape[-1] + margin - begin[2], source.shape[-1])
    shift_y = lax.rem(source.shape[-2] - begin[1], source.shape[-2])

    def cut(x, _):
        def take(ref, k):
            plane = pltpu.roll(ref[k, begin[0] + x], shift, 1)[:, :128]
            return pltpu.roll(plane, shift_y, 0)[:rows]

        for k in range(3):
            zone_u[k, x] = take(source, k)
            zone_f[k, x] = take(wide, 3 + k)
        zone_m[x] = take(wide, 6)
        return 0

    lax.fori_loop(0, count, cut, 0)


FIELDS = 8


def coarse_fields(zone_u, zone_f, zone_m, temp, fields):
    rows = zone_m.shape[1]
    first_y = iota((rows, 128), 0) % 2 == 1
    first_z = iota((rows, 128), 1) % 2 == 1
    rank = iota((PC, 128), 0)
    lane = iota((PC, 128), 1)
    for x in range(PC):
        for k in range(3):
            sums = [None] * FIELDS

            def put(number, value):
                sums[number] = value if sums[number] is None else sums[number] + value

            for a in range(2):
                at = 2 * x + 1 + a
                u, m = zone_u[k, at], zone_m[at]
                applied = MASS_TERM * u
                laplace = jnp.zeros_like(u)
                for number, (axis, step) in enumerate(
                    ((0, 1), (0, -1), (1, 1), (1, -1), (2, 1), (2, -1))
                ):
                    if axis == 0:
                        u_next, m_next = zone_u[k, at + step], zone_m[at + step]
                    else:
                        u_next, m_next = roll(u, -step, axis - 1), roll(m, -step, axis - 1)
                    change = u - u_next
                    applied = applied + 0.5 * (m + m_next) * change
                    laplace = laplace + change
                    flow = -0.5 * m_next * change
                    if axis == 0:
                        same = (a == 0) == (step == 1)
                        put(0 if same else 1 + number, flow)
                    else:
                        first = first_y if axis == 1 else first_z
                        near = first if step == 1 else ~first
                        put(0, jnp.where(near, flow, 0.0))
                        put(1 + number, jnp.where(near, 0.0, flow))
                put(0, -0.5 * m * laplace)
                put(7, zone_f[k, at] - applied)
            for number in range(FIELDS):
                slot = temp.at[k * FIELDS + number]
                slot[...] = sums[number]
                pair = slot[pl.ds(1, PC, stride=2), :] + slot[pl.ds(2, PC, stride=2), :]
                pair = pair + roll(pair, -1, 1)
                keep = (lane % 2 == 1) & (lane < 2 * PC)
                if number == 1 and x == PC - 1 or number == 2 and x == 0:
                    keep = jnp.zeros_like(keep)
                if number == 3:
                    keep = keep & (rank < PC - 1)
                if number == 4:
                    keep = keep & (rank > 0)
                if number == 5:
                    keep = keep & (lane < 2 * PC - 2)
                if number == 6:
                    keep = keep & (lane > 1)
                fields[k * FIELDS + number, x * PC : (x + 1) * PC, :] = jnp.where(keep, pair, 0.0)


def assemble(fields, strip, mat, side):
    size = fields.shape[1]
    gap = iota((size, 128), 1) - iota((size, 128), 0)
    mat[...] = jnp.zeros_like(mat)
    side[...] = jnp.zeros_like(side)
    for c in range(2):
        for t in range(PC // 2):
            z = t if c == 0 else PC - 1 - t
            for k in range(3):
                def column(number):
                    value = fields[k * FIELDS + number, :, 2 * z + 1 : 2 * z + 2]
                    return jnp.broadcast_to(value, (size, 128))

                part = slice(k * size, (k + 1) * size)
                ahead, behind = (5, 6) if c == 0 else (6, 5)
                strip[part, 0:128] = jnp.where(gap == 0, column(behind), 0.0)
                inner = jnp.where(gap == 0, column(0), 0.0)
                for number, offset in ((1, PC), (2, -PC), (3, 1), (4, -1)):
                    inner = jnp.where(gap == offset, column(number), inner)
                strip[part, 128:256] = inner
                strip[part, 256:384] = jnp.where(gap == 0, column(ahead), 0.0)
                strip[part, 384:512] = column(7)
            product = dot(strip[:, :384], strip[...], (0, 0))
            for i in range(3):
                at = t - 1 + i
                if at < 0:
                    continue
                rows = slice(128 * i, 128 * (i + 1))
                mat[c, at] += product[rows, 128 * i : 128 * (i + 1)]
                for j in range(i + 1, 3):
                    place = slice(128 * (j - i - 1), 128 * (j - i))
                    side[c, at, :, place] += product[rows, 128 * j : 128 * (j + 1)]
                side[c, at, :, 256:384] += product[rows, 384:512]


def inverted(blocks, count):
    row_at = iota(blocks[0].shape, 0)
    lane_at = iota((1, blocks[0].shape[1]), 1)
    for j in range(count):
        done = []
        for block in blocks:
            column = block[:, j : j + 1]
            row = block[j : j + 1, :]
            pivot = 1.0 / row[:, j : j + 1]
            row = jnp.where(lane_at == j, pivot, row * pivot)
            clear = (row_at == j) | (lane_at == j)
            column = jnp.where(row_at == j, -1.0, column)
            done.append(jnp.where(clear, 0.0, block) - column * row)
        blocks = done
    return blocks


def eliminate(t, chains, size, ridge, mat, side, solved):
    params = PC * PC
    diagonal = (iota((size, 128), 0) == iota((size, 128), 1)) & (iota((size, 128), 0) < params)
    blocks = [mat[c, t, :size, :] + jnp.where(diagonal, ridge, 0.0) for c in chains]
    for c, inverse in zip(chains, inverted(blocks, params)):
        right = side[c, t]
        w = dot(inverse, right, (1, 0))
        solved[c, t] = w
        schur = dot(right[:size, :256], w, (0, 0))
        mat[c, t + 1] -= schur[:128, :128]
        side[c, t + 1, :, 0:128] -= schur[:128, 128:256]
        side[c, t + 1, :, 256:384] -= schur[:128, 256:384]
        mat[c, t + 2] -= schur[128:, 128:256]
        side[c, t + 2, :, 256:384] -= schur[128:, 256:384]


def solve_zone(fields, mat, side, solved, answer):
    size = fields.shape[1]
    squares = jnp.zeros((size, 128), F32)
    for number in range(3 * FIELDS):
        if number % FIELDS < FIELDS - 1:
            squares = squares + fields[number] * fields[number]
    trace = jnp.sum(jnp.sum(squares, axis=0, keepdims=True), axis=1, keepdims=True)
    ridge = DAMPING * trace / PC**3 + EPSILON
    meet = PC // 2 - 1

    def both(t, _):
        eliminate(t, (0, 1), size, ridge, mat, side, solved)
        return 0

    lax.fori_loop(0, meet, both, 0)
    mat[0, meet] += mat[1, meet + 1]
    mat[0, meet + 1] += mat[1, meet]
    side[0, meet, :, 0:128] += side[1, meet, :, 0:128].T
    side[0, meet, :, 256:384] += side[1, meet + 1, :, 256:384]
    side[0, meet + 1, :, 256:384] += side[1, meet, :, 256:384]

    def single(t, _):
        eliminate(t, (0,), size, ridge, mat, side, solved)
        return 0

    lax.fori_loop(meet, meet + 2, single, 0)
    answer[...] = jnp.zeros_like(answer)

    def back(t, c):
        value = solved[c, t, :, 256:384]
        value = value - dot(solved[c, t, :, 0:128], answer[c, t + 1], (1, 0))
        value = value - dot(solved[c, t, :, 128:256], answer[c, t + 2], (1, 0))
        answer[c, t, :size, :] = value

    answer[0, meet + 1, :size, :] = solved[0, meet + 1, :, 256:384]
    value = solved[0, meet, :, 256:384]
    answer[0, meet, :size, :] = value - dot(solved[0, meet, :, 0:128], answer[0, meet + 1], (1, 0))
    answer[1, meet] = answer[0, meet + 1]
    answer[1, meet + 1] = answer[0, meet]
    for t in range(meet - 1, -1, -1):
        for c in range(2):
            back(t, c)


def place_zone(begin, zone_m, answer, spread, temp, added):
    rows = zone_m.shape[1]
    span = 2 * PC
    lane = iota((128, 128), 1)
    update = jnp.zeros((128, 128), F32)
    for z in range(PC):
        value = answer[0, z] if z < PC // 2 else answer[1, PC - 1 - z]
        update = jnp.where((lane == 2 * z + 1) | (lane == 2 * z + 2), -value, update)
    spread[...] = update

    def ramp(position):
        value = jnp.sin(math.pi * (position.astype(F32) - 0.5) / span)
        return jnp.where((position >= 1) & (position <= span), value, 0.0)

    weight = ramp(iota((rows, 128), 0)) * ramp(iota((rows, 128), 1))
    temp[0] = jnp.zeros_like(weight)
    for x in range(PC):
        part = spread[x * PC : (x + 1) * PC, :]
        temp[0, pl.ds(1, PC, stride=2), :] = part
        temp[0, pl.ds(2, PC, stride=2), :] = part
        value = weight * temp[0]
        for a in range(2):
            at = 2 * x + 1 + a
            plane = value * math.sin(math.pi * (at - 0.5) / span) * zone_m[at]
            plane = jnp.pad(plane, ((0, added.shape[1] - rows), (0, 0)))
            plane = pltpu.roll(plane, begin[1] - FSWEEPS, 0)
            plane = jnp.pad(plane, ((0, 0), (0, added.shape[2] - 128)))
            plane = pltpu.roll(plane, begin[2] - FSWEEPS, 1)
            added[begin[0] - FSWEEPS + at] += plane


def pack_kernel(margin, across, low_out, high_out):
    channels, span_x, rows, lanes = across.shape
    room = 128 // margin
    lane = iota((rows, 128), 1)

    def pack(k, _):
        for group in range(low_out.shape[1]):
            low = high = jnp.zeros((rows, 128), F32)
            for j in range(min(room, span_x - group * room)):
                x = group * room + j
                here = (lane >= j * margin) & (lane < (j + 1) * margin)
                low = jnp.where(here, roll(across[k, x, :, :128], j * margin, 1), low)
                last = across[k, x, :, lanes - 128 :]
                high = jnp.where(here, roll(last, j * margin + margin, 1), high)
            low_out[k, group] = low
            high_out[k, group] = high
        return 0

    lax.fori_loop(0, channels, pack, 0)


def widen(margin, across, from_low, from_high, wide):
    channels, span_x, rows, lanes = across.shape
    room = 128 // margin
    lane = iota((rows, 128), 1)

    def spread(k, _):
        for x in range(span_x):
            group, j = x // room, x % room
            high = roll(from_high[k, group], -j * margin, 1)
            low = roll(from_low[k, group], -j * margin - margin, 1)
            halo = jnp.where(lane < margin, high, jnp.where(lane >= 128 - margin, low, 0.0))
            wide[k, x, :, :lanes] = across[k, x]
            wide[k, x, :, lanes:] = halo
        return 0

    lax.fori_loop(0, channels, spread, 0)


def kernel(totals, brick, margin, starts, across, from_low, from_high, field_out, added, wide, *scratch):
    widen(margin, across, from_low, from_high, wide)
    (buf_a, buf_b, mx, my, mz, inverse, zone_u, zone_f, zone_m) = scratch[:9]
    temp, fields, strip, mat, side, solved, answer, spread = scratch[9:]
    source = relax_planes(
        totals, brick, margin, wide, field_out, (buf_a, buf_b), (mx, my, mz, inverse)
    )
    added[...] = jnp.zeros_like(added)
    for number in range(starts.shape[0]):
        begin = [starts[number, axis] for axis in range(3)]
        cut_zone(begin, margin, source, wide, zone_u, zone_f, zone_m)
        fields[...] = jnp.zeros_like(fields)
        coarse_fields(zone_u, zone_f, zone_m, temp, fields)
        assemble(fields, strip, mat, side)
        solve_zone(fields, mat, side, solved, answer)
        place_zone(begin, zone_m, answer, spread, temp, added)


def exchange(first, last, axis):
    count = lax.axis_size(axis)
    forward = [(i, i + 1) for i in range(count - 1)]
    backward = [(target, source) for source, target in forward]
    return lax.ppermute(last, axis, forward), lax.ppermute(first, axis, backward)


def body(forcing, start_field, modulus, corners):
    brick = modulus.shape
    lower = [lax.axis_index(n) * size for n, size in zip(("gx", "gy", "gz"), brick)]
    totals = [lax.axis_size(n) * size for n, size in zip(("gx", "gy", "gz"), brick)]
    margin = HALO + FSWEEPS
    stacked = jnp.concatenate([start_field, forcing, modulus[None]], axis=0)
    channels = stacked.shape[0]
    x_low, x_high = exchange(stacked[:, :margin], stacked[:, -margin:], "gx")
    y_low, y_high = exchange(stacked[:, :, :margin], stacked[:, :, -margin:], "gy")
    sides = jnp.stack([y_low, y_high])
    low_ends, high_ends = exchange(sides[:, :, :margin], sides[:, :, -margin:], "gx")
    across = jnp.concatenate(
        [
            jnp.concatenate([low_ends[0], x_low, low_ends[1]], axis=2),
            jnp.concatenate([y_low, stacked, y_high], axis=2),
            jnp.concatenate([high_ends[0], x_high, high_ends[1]], axis=2),
        ],
        axis=1,
    )
    span_x, span_y = across.shape[1:3]
    rows, lanes = -(-span_y // 8) * 8, brick[2] + 128
    across = jnp.pad(across, ((0, 0), (0, 0), (0, rows - span_y), (0, 0)))
    groups = -(-span_x // (128 // margin))
    packed = jax.ShapeDtypeStruct((channels, groups, rows, 128), F32)
    whole = pl.BlockSpec(memory_space=pltpu.VMEM)
    limit = pltpu.CompilerParams(vmem_limit_bytes=56 * 1024 * 1024)
    z_low, z_high = pl.pallas_call(
        functools.partial(pack_kernel, margin),
        out_shape=(packed, packed),
        in_specs=[whole],
        out_specs=(whole, whole),
        compiler_params=limit,
    )(across)
    z_low, z_high = exchange(z_low, z_high, "gz")
    starts = (corners - jnp.stack(lower).astype(jnp.int32)[None, :] + margin - 1).astype(jnp.int32)
    zone_span = 2 * PC + 2
    zone_rows = -(-zone_span // 8) * 8
    size = -(-PC * PC // 8) * 8
    planes = PC // 2 + 3
    plane_buffer = pltpu.VMEM((span_x, rows, lanes), F32)
    reach = tuple(size + 2 * HALO for size in brick)
    field, added = pl.pallas_call(
        functools.partial(kernel, totals, brick, margin),
        out_shape=(
            jax.ShapeDtypeStruct(forcing.shape, F32),
            jax.ShapeDtypeStruct((reach[0], rows, lanes), F32),
        ),
        in_specs=[pl.BlockSpec(memory_space=pltpu.SMEM), whole, whole, whole],
        out_specs=(whole, whole),
        scratch_shapes=[
            pltpu.VMEM((channels, span_x, rows, lanes), F32),
            pltpu.VMEM((3, span_x, rows, lanes), F32),
            pltpu.VMEM((3, span_x, rows, lanes), F32),
            plane_buffer, plane_buffer, plane_buffer, plane_buffer,
            pltpu.VMEM((3, zone_span, zone_rows, 128), F32),
            pltpu.VMEM((3, zone_span, zone_rows, 128), F32),
            pltpu.VMEM((zone_span, zone_rows, 128), F32),
            pltpu.VMEM((3 * FIELDS, zone_rows, 128), F32),
            pltpu.VMEM((3 * FIELDS, size, 128), F32),
            pltpu.VMEM((3 * size, 512), F32),
            pltpu.VMEM((2, planes, 128, 128), F32),
            pltpu.VMEM((2, planes, 128, 384), F32),
            pltpu.VMEM((2, planes, size, 384), F32),
            pltpu.VMEM((2, planes, 128, 128), F32),
            pltpu.VMEM((128, 128), F32),
        ],
        compiler_params=limit,
    )(starts, across, z_low, z_high)
    summed = added[:, : reach[1], : reach[2]]
    received = extended(pack_margins(summed, 0, HALO), (("gx", 0),), HALO)
    summed = fold_margins(summed, received, 0, HALO)
    received = extended(pack_margins(summed, 1, HALO), (("gy", 1),), HALO)
    summed = fold_margins(summed, received, 1, HALO)
    received = extended(pack_margins(summed, 2, HALO), (("gz", 2),), HALO)
    summed = fold_margins(summed, received, 2, HALO)
    return (field, modulus + summed)


def solution(mesh):
    placed = (
        P(None, "gx", "gy", "gz"),
        P(None, "gx", "gy", "gz"),
        P("gx", "gy", "gz"),
        P(("gx", "gy", "gz"), None),
    )
    return jax.shard_map(
        body,
        mesh=mesh,
        in_specs=placed,
        out_specs=(P(None, "gx", "gy", "gz"), P("gx", "gy", "gz")),
        check_vma=False,
    )
```
